32 devices in a mesh: grp: 2 (over y), pos: 16 (over z, x, core).
Axes of the slice: x: 2, y: 2, z: 4, core: 2. Of those that a mesh axis runs over, the one named last changes fastest.
Arguments:
- object_field: float32 [2, 2048, 2048], P(None, 'grp', 'pos'), may hold values from -5 to 5
- probe_field: float32 [2, 256, 256], replicated, may hold values from -5 to 5
- patterns: float32 [96, 256, 256], P(('grp', 'pos')), may hold values from 0.05 to 5
- corners: int32 [2, 96], P(None, ('grp', 'pos')), may hold values from 0 to 1792, as said below
- counts: int32 [32], replicated, may hold values from 1 to 3, as said below
Outputs:
- object_new: float32 [2, 2048, 2048], P(None, 'grp', 'pos')
- probe_new: float32 [2, 256, 256], replicated
The draws below stay inside these ranges and needn't reach their ends.
Inputs may be any that keep to these rules, and one draw needn't show every extreme that they name: `corners`: each slot's patch of 256 x 256 cells lies inside the object and inside its device's block of 1024 x 128 object cells extended by 128 cells on every side (the device at grp index a and pos index b holds rows a * 1024 to a * 1024 + 1023 and columns b * 128 to b * 128 + 127). The live slots of a device are its first counts[d] slots; some device has all 3 slots live.
All inputs are finite; a program needn't handle non-finite values.
Results may differ from the reference program's by a relative error of at most 0.00012.
Values sent between devices are 32-bit elements; how exact they have to be, the bound alone decides.
A program may use at most 64 MiB of HBM per device.

```python
import math
import jax
import jax.numpy as jnp
from jax import lax

M = 256
TR = 1024
TC = 128
HALO = 128
CAP = 3
NR = 2048
NC = 2048
SLOTS = 96
DEVICES = 32


def draw_corners(key, part):
    row_key, col_key = jax.random.split(key, 2)
    device = jnp.arange(SLOTS, dtype=jnp.int32) // CAP
    along = NC // TC
    grp_index = device // along
    pos_index = device % along
    row_low = jnp.maximum(0, grp_index * TR - HALO)
    row_high = jnp.minimum(NR - M, grp_index * TR + TR + HALO - M)
    col_low = jnp.maximum(0, pos_index * TC - HALO)
    col_high = jnp.minimum(NC - M, pos_index * TC + TC + HALO - M)
    rows = jax.random.randint(row_key, (SLOTS,), row_low, row_high + 1)
    cols = jax.random.randint(col_key, (SLOTS,), col_low, col_high + 1)
    last_first = SLOTS - CAP
    rows = rows.at[0].set(row_low[0]).at[last_first].set(row_high[last_first])
    cols = cols.at[0].set(col_low[0]).at[last_first].set(col_high[last_first])
    return jnp.stack((rows, cols)).astype(jnp.int32)


def draw_counts(key, part):
    base_key, hot_key, pick_key = jax.random.split(key, 3)
    base = jax.random.randint(base_key, (DEVICES,), 1, CAP // 2 + 1)
    hot = jax.random.randint(hot_key, (DEVICES,), 0, 8) == 0
    chosen = jnp.arange(DEVICES) == jax.random.randint(pick_key, (), 0, DEVICES)
    return jnp.where(hot | chosen, CAP, base).astype(jnp.int32)


def level_of(rng, dims, pieces, low, high):
    def one(dim, blocks):
        heights = jax.random.uniform(jax.random.fold_in(jax.random.fold_in(rng, 6), dim), (blocks,), jnp.float32, low / len(pieces), high / len(pieces))
        return jnp.repeat(jnp.exp(heights), dims[dim] // blocks).reshape((-1,) + (1,) * (len(dims) - dim - 1))

    loudness = one(*pieces[0])
    for cut in pieces[1:]:
        loudness = loudness * one(*cut)
    return loudness


def gaussian(stream_key, dims, deviation, bound, cuts=(), held_as=jnp.bfloat16):
    array = deviation * jax.random.normal(stream_key, dims, jnp.float32)
    if cuts:
        array = array * level_of(stream_key, dims, cuts, -0.22, 0.18)
    return jnp.clip(array, -bound, bound).astype(held_as)


def setup_inputs(seed: int = 0) -> dict:
    keys = jax.random.split(jax.random.key(seed), 6)
    return {
        "object_field": gaussian(keys[0], (2, NR, NC), 0.7, 5.0, ((1, 2), (2, 16)), jnp.float32),
        "probe_field": gaussian(keys[1], (2, M, M), 0.7, 5.0, (), jnp.float32),
        "patterns": jnp.clip(jnp.exp(math.log(5.0) - 4.6051702 * jax.random.uniform(keys[2], (SLOTS, M, M), jnp.float32) ** level_of(keys[2], (SLOTS, M, M), ((0, 32),), -0.2, 0.2)), 0.05, 5.0),
        "corners": draw_corners(jax.random.fold_in(keys[5], 71), 0),
        "counts": draw_counts(jax.random.fold_in(keys[5], 71), 0),
    }


def residual_wave(probe_field, patch_field, measured):
    wave = (probe_field[0] * patch_field[0] - probe_field[1] * patch_field[1]) + 1j * (probe_field[0] * patch_field[1] + probe_field[1] * patch_field[0])
    far = jnp.fft.fft2(wave, norm="ortho")
    excess = jnp.real(far) ** 2 + jnp.imag(far) ** 2 - measured
    back = jnp.fft.ifft2(excess * far, norm="ortho")
    return jnp.real(back), jnp.imag(back)


def reference(object_field, probe_field, patterns, corners, counts):
    slot_total = patterns.shape[0]
    per_device = slot_total // counts.shape[0]

    def visit_slot(index, totals):
        grad_object, grad_probe = totals
        owner = (index // per_device).astype(jnp.int32)
        is_live = (index % per_device) < counts[owner]
        weight = jnp.where(is_live, jnp.float32(1.0), jnp.float32(0.0))
        row_at = corners[0, index].astype(jnp.int32)
        col_at = corners[1, index].astype(jnp.int32)
        anchor = (jnp.int32(0), row_at, col_at)
        patch_field = lax.dynamic_slice(object_field, anchor, (2, M, M))
        chi_re, chi_im = residual_wave(probe_field, patch_field, patterns[index])
        chi_re = chi_re.astype(jnp.float32) * weight
        chi_im = chi_im.astype(jnp.float32) * weight
        obj_re = probe_field[0] * chi_re + probe_field[1] * chi_im
        obj_im = probe_field[0] * chi_im - probe_field[1] * chi_re
        prb_re = patch_field[0] * chi_re + patch_field[1] * chi_im
        prb_im = patch_field[0] * chi_im - patch_field[1] * chi_re
        current = lax.dynamic_slice(grad_object, anchor, (2, M, M))
        grad_object = lax.dynamic_update_slice(grad_object, current + jnp.stack((obj_re, obj_im)), anchor)
        return grad_object, grad_probe + jnp.stack((prb_re, prb_im))

    start_totals = (jnp.zeros(object_field.shape, jnp.float32), jnp.zeros(probe_field.shape, jnp.float32))
    grad_object, grad_probe = lax.fori_loop(0, slot_total, visit_slot, start_totals)
    live_total = jnp.sum(counts).astype(jnp.float32)
    object_new = object_field - 0.25 * grad_object
    probe_new = probe_field - 4.0 * grad_probe / live_total
    return object_new, probe_new
```

```python
import functools

import jax
import jax.numpy as jnp
import numpy as np
from jax import lax
from jax.experimental import pallas as pl
from jax.experimental.pallas import tpu as pltpu
from jax.sharding import PartitionSpec as P

HALO = 128
STEP_OBJECT = 0.25
STEP_PROBE = 4.0
MESH = pl.DeviceIdType.MESH


def dft_tables(order):
    indices = np.arange(order, dtype=np.int64)
    angles = (indices[:, None] * indices[None, :] % order) * (2.0 * np.pi / order)
    cos = np.cos(angles) / np.sqrt(order)
    sin = -np.sin(angles) / np.sqrt(order)
    left = np.block([[cos, -sin], [sin, cos]])
    right = np.block([[cos, sin], [-sin, cos]])
    both = np.stack([left, right]).astype(np.float32)
    high = both.astype(jnp.bfloat16)
    low = (both - high.astype(np.float32)).astype(jnp.bfloat16)
    return np.stack([high, low], axis=1)


def split(x):
    high = x.astype(jnp.bfloat16)
    low = (x - high.astype(jnp.float32)).astype(jnp.bfloat16)
    return high, low


def dot(a, b):
    return jnp.dot(a, b, preferred_element_type=jnp.float32)


def table_left(tab, which, data):
    high, low = split(data)
    th, tl = tab[which, 0], tab[which, 1]
    return dot(th, high) + (dot(th, low) + dot(tl, high))


def table_right(data, tab, which):
    high, low = split(data)
    th, tl = tab[which, 0], tab[which, 1]
    return dot(high, th) + (dot(low, th) + dot(high, tl))


def kernel(sizes, corners, counts, obj_hbm, prb_hbm, pat_hbm, tab_hbm, obj_out, prb_out,
           ext, prb, pat, tab, nb, stage, corv, cor_recv, cor_smem,
           gmid, gsend, grecv, gacc, yrecv, gp, p1r, p1, p2r, p2, p3r, pnew,
           loc, yh, corsem, cors, patsem, gsem, ysem, csem, gysem, asem, agsem, gasem, casem):
    G, PN, S, TR, M = sizes
    grp, pos = lax.axis_index("grp"), lax.axis_index("pos")
    core, chip, chips = lax.rem(pos, 2), pos // 2, PN // 2
    half = M // 2
    h2 = half // G
    h3 = max(8, h2 // chips)
    owners = h2 // h3

    def at(g, p):
        return {"device_id": (g, p), "device_id_type": MESH}

    col_peer = [at(grp, lax.rem(pos + PN - 1, PN)), at(grp, lax.rem(pos + 1, PN))]
    row_peer = [at(lax.rem(grp + G - 1, G), pos), at(lax.rem(grp + 1, G), pos)]
    col_send, col_recv = [pos > 0, pos < PN - 1], [pos < PN - 1, pos > 0]
    row_send, row_recv = [grp > 0, grp < G - 1], [grp < G - 1, grp > 0]
    partner = at(grp, pos + 1 - 2 * core)

    def grp_at(k):
        return lax.rem(grp + k, G)

    def chip_at(k):
        return lax.rem(chip + k, chips)

    locals_ = [
        pltpu.make_async_copy(obj_hbm, ext.at[:, pl.ds(HALO, TR), :], loc.at[0]),
        pltpu.make_async_copy(prb_hbm, prb, loc.at[1]),
        pltpu.make_async_copy(pat_hbm, pat, loc.at[2]),
        pltpu.make_async_copy(tab_hbm, tab, loc.at[3]),
    ]
    for c in locals_:
        c.start()

    barrier = pltpu.get_barrier_semaphore()
    for d in range(2):
        @pl.when(col_send[d])
        def _():
            pl.semaphore_signal(barrier, inc=1, **col_peer[d])
    for k in range(1, G):
        pl.semaphore_signal(barrier, inc=1, **at(grp_at(k), pos))
    for k in range(1, chips):
        pl.semaphore_signal(barrier, inc=1, **at(grp, chip_at(k) * 2 + core))
    pl.semaphore_signal(barrier, inc=1, **partner)
    expected = (pos > 0).astype(jnp.int32) + (pos < PN - 1).astype(jnp.int32) + G + chips - 1

    lane = lax.broadcasted_iota(jnp.int32, (M, HALO), 1)
    row8 = lax.broadcasted_iota(jnp.int32, (8, 128), 0)
    packed = jnp.zeros((8, 128), jnp.int32)
    for s in range(S):
        packed = jnp.where(row8 == s, corners[0, s] - grp * TR + HALO, packed)
    corv[...] = packed
    zero = jnp.zeros((HALO, HALO), jnp.float32)
    for s in range(S):
        for c in range(2):
            for at_row in (0, HALO + M):
                gmid[s, c, pl.ds(at_row, HALO), :] = zero
                for d in range(2):
                    grecv[d, s, c, pl.ds(at_row, HALO), :] = zero
    gp[...] = jnp.zeros(gp.shape, jnp.float32)

    pl.semaphore_wait(barrier, expected)

    def cor_copy(d):
        return pltpu.make_async_remote_copy(corv, cor_recv.at[d], corsem.at[0, d], corsem.at[1, d], **col_peer[d])

    def halo_copy(d):
        src, dst = ((0, HALO + TR), (TR - HALO, 0))[d]
        return pltpu.make_async_remote_copy(
            obj_hbm.at[:, pl.ds(src, HALO), :], ext.at[:, pl.ds(dst, HALO), :], yh.at[0, d], yh.at[1, d], **row_peer[d])

    for d in range(2):
        @pl.when(col_send[d])
        def _():
            cor_copy(d).start()

        @pl.when(row_send[d])
        def _():
            halo_copy(d).start()
    for d in range(2):
        @pl.when(col_recv[d])
        def _():
            cor_copy(d).wait_recv()
            c = pltpu.make_async_copy(cor_recv.at[d], cor_smem.at[d], cors.at[d])
            c.start()
            c.wait()
    locals_[0].wait()
    for d in range(2):
        @pl.when(row_recv[d])
        def _():
            halo_copy(d).wait_recv()

    def patch_copy(d, s):
        return pltpu.make_async_remote_copy(
            stage.at[d, s], nb.at[d, s], patsem.at[0, d, s], patsem.at[1, d, s], **col_peer[d])

    def grad_copy(d, s):
        return pltpu.make_async_remote_copy(
            gsend.at[d, s], grecv.at[d, s, :, pl.ds(HALO, M), :], gsem.at[0, d, s], gsem.at[1, d, s], **col_peer[d])

    for s in range(S):
        for d in range(2):
            @pl.when(col_send[d])
            def _():
                r = jnp.clip(cor_smem[1 - d, s, 0], 0, TR + 2 * HALO - M)
                for c in range(2):
                    stage[d, s, c] = ext[c, pl.ds(r, M), :]
                patch_copy(d, s).start()

    for c in locals_[1:]:
        c.wait()
    own_count = counts[grp * PN + pos]

    def slot(s, carry):
        r = jnp.clip(corners[0, s] - grp * TR + HALO, 0, TR + 2 * HALO - M)
        shift = jnp.clip(corners[1, s] - pos * HALO + HALO, 0, HALO)
        for d in range(2):
            @pl.when(col_recv[d])
            def _():
                patch_copy(d, s).wait_recv()
        back = lax.rem(HALO - shift, HALO)
        forth = lax.rem(shift, HALO)
        first = lane < HALO - shift
        patch = []
        for c in range(2):
            mid = pltpu.roll(ext[c, pl.ds(r, M), :], back, 1)
            before = pltpu.roll(nb[1, s, c], back, 1)
            after = pltpu.roll(nb[0, s, c], back, 1)
            patch.append(jnp.concatenate([jnp.where(first, before, mid), jnp.where(first, mid, after)], axis=1))
        pr, pi = prb[0], prb[1]
        wave = jnp.concatenate([pr * patch[0] - pi * patch[1], pr * patch[1] + pi * patch[0]], axis=0)
        front = table_left(tab, 0, wave)
        far = table_right(jnp.concatenate([front[:M], front[M:]], axis=1), tab, 1)
        fr, fi = far[:, :M], far[:, M:]
        excess = fr * fr + fi * fi - pat[s]
        excess = jnp.where(jnp.full((M, M), s, jnp.int32) < own_count, excess, 0.0)
        back_ = table_left(tab, 1, jnp.concatenate([excess * fr, excess * fi], axis=0))
        chi = table_right(jnp.concatenate([back_[:M], back_[M:]], axis=1), tab, 0)
        cr, ci = chi[:, :M], chi[:, M:]
        parts = (pr * cr + pi * ci, pr * ci - pi * cr)
        gp[0] += patch[0] * cr + patch[1] * ci
        gp[1] += patch[0] * ci - patch[1] * cr
        tail = lane >= shift
        for c in range(2):
            g0 = pltpu.roll(parts[c][:, :HALO], forth, 1)
            g1 = pltpu.roll(parts[c][:, HALO:], forth, 1)
            gsend[0, s, c] = jnp.where(tail, g0, 0.0)
            gmid[s, c, pl.ds(HALO, M), :] = jnp.where(tail, g1, g0)
            gsend[1, s, c] = jnp.where(tail, 0.0, g1)
        for d in range(2):
            @pl.when(col_send[d])
            def _():
                grad_copy(d, s).start()
        return carry

    lax.fori_loop(0, S, slot, 0)

    core_copy = pltpu.make_async_remote_copy(
        gp.at[:, pl.ds((1 - core) * half, half), :], p1r, csem.at[0], csem.at[1], **partner)
    core_copy.start()
    core_copy.wait_recv()
    p1[...] = gp[:, pl.ds(pl.multiple_of(core * half, half), half), :] + p1r[...]

    def grp_copy(k):
        rows = pl.ds(pl.multiple_of(grp_at(k) * h2, h2), h2)
        return pltpu.make_async_remote_copy(
            p1.at[:, rows, :], p2r.at[k], gysem.at[0, k], gysem.at[1, k], **at(grp_at(k), pos))

    for k in range(1, G):
        grp_copy(k).start()

    for s in range(S):
        for d in range(2):
            @pl.when(col_recv[d])
            def _():
                grad_copy(d, s).wait_recv()

    def gather(chunk, carry):
        base = pl.multiple_of(chunk * HALO, HALO)
        totals = [jnp.zeros((HALO, HALO), jnp.float32)] * 2
        for s in range(S):
            off = jnp.clip(base - (corners[0, s] - grp * TR + HALO) + HALO, 0, HALO + M)
            totals = [totals[c] + gmid[s, c, pl.ds(off, HALO), :] for c in range(2)]
        for c in range(2):
            gacc[c, pl.ds(base, HALO), :] = totals[c]
        for d in range(2):
            @pl.when(col_recv[d])
            def _():
                for c in range(2):
                    total = gacc[c, pl.ds(base, HALO), :]
                    for s in range(S):
                        off = jnp.clip(base - cor_smem[d, s, 0] + HALO, 0, HALO + M)
                        total = total + grecv[d, s, c, pl.ds(off, HALO), :]
                    gacc[c, pl.ds(base, HALO), :] = total
        return carry

    lax.fori_loop(0, (TR + 2 * HALO) // HALO, gather, 0)

    def rim_copy(d):
        src = (0, HALO + TR)[d]
        return pltpu.make_async_remote_copy(
            gacc.at[:, pl.ds(src, HALO), :], yrecv.at[d], ysem.at[0, d], ysem.at[1, d], **row_peer[d])

    for d in range(2):
        @pl.when(row_send[d])
        def _():
            rim_copy(d).start()

    for k in range(1, G):
        grp_copy(k).wait_recv()
    total = p1[:, pl.ds(pl.multiple_of(grp * h2, h2), h2), :]
    for k in range(1, G):
        total = total + p2r[k]
    p2[...] = total

    def share_copy(k):
        q = lax.rem(chip_at(k), owners)
        rows = pl.ds(pl.multiple_of(q * h3, 8), h3)
        return pltpu.make_async_remote_copy(
            p2.at[:, rows, :], p3r.at[k], asem.at[0, k], asem.at[1, k], **at(grp, chip_at(k) * 2 + core))

    for k in range(1, chips):
        @pl.when(chip_at(k) < owners)
        def _():
            share_copy(k).start()

    obj_out[...] = ext[:, pl.ds(HALO, TR), :] - STEP_OBJECT * gacc[:, pl.ds(HALO, TR), :]
    for d in range(2):
        @pl.when(row_recv[d])
        def _():
            rim_copy(d).wait_recv()
            rows = pl.ds((TR - HALO, 0)[d], HALO)
            obj_out[:, rows, :] = obj_out[:, rows, :] - STEP_OBJECT * yrecv[d]

    live = counts[0]
    for i in range(1, G * PN):
        live = live + counts[i]

    def new_rows(owner):
        return pl.ds(pl.multiple_of(core * half + grp * h2 + lax.rem(owner, owners) * h3, 8), h3)

    @pl.when(chip < owners)
    def _():
        total = p2[:, pl.ds(pl.multiple_of(lax.rem(chip, owners) * h3, 8), h3), :]
        for k in range(1, chips):
            share_copy(k).wait_recv()
            total = total + p3r[k]
        divisor = jnp.full(total.shape, live, jnp.int32).astype(jnp.float32)
        pnew[:, new_rows(chip), :] = prb[:, new_rows(chip), :] - STEP_PROBE * total / divisor

    def spread_copy(k, owner):
        return pltpu.make_async_remote_copy(
            pnew.at[:, new_rows(owner), :], pnew.at[:, new_rows(owner), :], agsem.at[0, k], agsem.at[1, k],
            **at(grp, chip_at(k) * 2 + core))

    @pl.when(chip < owners)
    def _():
        for k in range(1, chips):
            spread_copy(k, chip).start()
    for k in range(1, chips):
        source = lax.rem(chip + chips - k, chips)

        @pl.when(source < owners)
        def _():
            spread_copy(k, source).wait_recv()

    def grp_spread(k, g):
        rows = pl.ds(pl.multiple_of(core * half + g * h2, h2), h2)
        return pltpu.make_async_remote_copy(
            pnew.at[:, rows, :], pnew.at[:, rows, :], gasem.at[0, k], gasem.at[1, k], **at(grp_at(k), pos))

    for k in range(1, G):
        grp_spread(k, grp).start()
    for k in range(1, G):
        grp_spread(k, lax.rem(grp + G - k, G)).wait_recv()

    def core_spread(c):
        rows = pl.ds(pl.multiple_of(c * half, half), half)
        return pltpu.make_async_remote_copy(pnew.at[:, rows, :], pnew.at[:, rows, :], casem.at[0], casem.at[1], **partner)

    core_spread(core).start()
    core_spread(1 - core).wait_recv()
    prb_out[...] = pnew[...]

    for d in range(2):
        @pl.when(col_send[d])
        def _():
            cor_copy(d).wait_send()
            for s in range(S):
                patch_copy(d, s).wait_send()
                grad_copy(d, s).wait_send()

        @pl.when(row_send[d])
        def _():
            halo_copy(d).wait_send()
            rim_copy(d).wait_send()
    core_copy.wait_send()
    for k in range(1, G):
        grp_copy(k).wait_send()
        grp_spread(k, grp).wait_send()
    for k in range(1, chips):
        @pl.when(chip_at(k) < owners)
        def _():
            share_copy(k).wait_send()

        @pl.when(chip < owners)
        def _():
            spread_copy(k, chip).wait_send()
    core_spread(core).wait_send()


def on_device(grp_size, pos_size, tables, object_field, probe_field, patterns, corners, counts):
    TR, S, M = object_field.shape[1], patterns.shape[0], probe_field.shape[1]
    chips, half = pos_size // 2, M // 2
    h2 = half // grp_size
    h3 = max(8, h2 // chips)
    f32 = jnp.float32
    V, D = pltpu.VMEM, pltpu.SemaphoreType.DMA
    smem = pl.BlockSpec(memory_space=pltpu.SMEM)
    hbm = pl.BlockSpec(memory_space=pl.ANY)
    vmem = pl.BlockSpec(memory_space=pltpu.VMEM)
    return pl.pallas_call(
        functools.partial(kernel, (grp_size, pos_size, S, TR, M)),
        out_shape=(
            jax.ShapeDtypeStruct(object_field.shape, f32),
            jax.ShapeDtypeStruct(probe_field.shape, f32),
        ),
        in_specs=[smem, smem, hbm, hbm, hbm, hbm],
        out_specs=(vmem, vmem),
        scratch_shapes=[
            V((2, TR + 2 * HALO, HALO), f32),
            V((2, M, M), f32),
            V((S, M, M), f32),
            V(tables.shape, jnp.bfloat16),
            V((2, S, 2, M, HALO), f32),
            V((2, S, 2, M, HALO), f32),
            V((8, 128), jnp.int32),
            V((2, 8, 128), jnp.int32),
            pltpu.SMEM((2, 8, 128), jnp.int32),
            V((S, 2, M + 2 * HALO, HALO), f32),
            V((2, S, 2, M, HALO), f32),
            V((2, S, 2, M + 2 * HALO, HALO), f32),
            V((2, TR + 2 * HALO, HALO), f32),
            V((2, 2, HALO, HALO), f32),
            V((2, M, M), f32),
            V((2, half, M), f32),
            V((2, half, M), f32),
            V((grp_size, 2, h2, M), f32),
            V((2, h2, M), f32),
            V((chips, 2, h3, M), f32),
            V((2, M, M), f32),
            D((4,)), D((2, 2)), D((2, 2)), D((2,)), D((2, 2, S)), D((2, 2, S)), D((2, 2)), D((2,)),
            D((2, grp_size)), D((2, chips)), D((2, chips)), D((2, grp_size)), D((2,)),
        ],
        compiler_params=pltpu.CompilerParams(
            collective_id=0, has_side_effects=True, vmem_limit_bytes=56 * 1024 * 1024
        ),
    )(corners, counts, object_field, probe_field, patterns, jnp.asarray(tables))


def solution(mesh):
    def body(object_field, probe_field, patterns, corners, counts):
        tables = dft_tables(probe_field.shape[1])
        return on_device(
            mesh.shape["grp"], mesh.shape["pos"], tables, object_field, probe_field, patterns, corners, counts
        )

    return jax.shard_map(
        body,
        mesh=mesh,
        in_specs=(
            P(None, "grp", "pos"),
            P(),
            P(("grp", "pos"), None, None),
            P(None, ("grp", "pos")),
            P(),
        ),
        out_specs=(P(None, "grp", "pos"), P()),
        check_vma=False,
    )
```

```python
import functools

import jax
import jax.numpy as jnp
import numpy as np
from jax import lax
from jax.experimental import pallas as pl
from jax.experimental.pallas import tpu as pltpu
from jax.sharding import PartitionSpec as P

HALO = 128
STEP_OBJECT = 0.25
STEP_PROBE = 4.0
MESH = pl.DeviceIdType.MESH


def dft_tables(order):
    indices = np.arange(order, dtype=np.int64)
    angles = (indices[:, None] * indices[None, :] % order) * (2.0 * np.pi / order)
    cos = np.cos(angles) / np.sqrt(order)
    sin = -np.sin(angles) / np.sqrt(order)
    left = np.block([[cos, -sin], [sin, cos]])
    right = np.block([[cos, sin], [-sin, cos]])
    both = np.stack([left, right]).astype(np.float32)
    high = both.astype(jnp.bfloat16)
    low = (both - high.astype(np.float32)).astype(jnp.bfloat16)
    return np.stack([high, low], axis=1)


def split(x):
    high = x.astype(jnp.bfloat16)
    low = (x - high.astype(jnp.float32)).astype(jnp.bfloat16)
    return high, low


def dot(a, b):
    return jnp.dot(a, b, preferred_element_type=jnp.float32)


def table_left(tab, which, data):
    high, low = split(data)
    th, tl = tab[which, 0], tab[which, 1]
    return dot(th, high) + (dot(th, low) + dot(tl, high))


def table_right(data, tab, which):
    high, low = split(data)
    th, tl = tab[which, 0], tab[which, 1]
    return dot(high, th) + (dot(low, th) + dot(high, tl))


def kernel(sizes, corners, counts, obj_hbm, prb_hbm, pat_hbm, tab_hbm, obj_out, prb_out,
           ext, prb, pat, tab, nb, stage, corv, cor_recv, cor_smem,
           gmid, gsend, grecv, gacc, yrecv, gp, p1r, p1, p2r, p2, p3r, pnew,
           loc, yh, corsem, cors, patsem, gsem, ysem, csem, gysem, asem, agsem, gasem, casem):
    G, PN, S, TR, M = sizes
    grp, pos = lax.axis_index("grp"), lax.axis_index("pos")
    core, chip, chips = lax.rem(pos, 2), pos // 2, PN // 2
    half = M // 2
    h2 = half // G
    h3 = max(8, h2 // chips)
    owners = h2 // h3

    def at(g, p):
        return {"device_id": (g, p), "device_id_type": MESH}

    col_peer = [at(grp, lax.rem(pos + PN - 1, PN)), at(grp, lax.rem(pos + 1, PN))]
    row_peer = [at(lax.rem(grp + G - 1, G), pos), at(lax.rem(grp + 1, G), pos)]
    col_send, col_recv = [pos > 0, pos < PN - 1], [pos < PN - 1, pos > 0]
    row_send, row_recv = [grp > 0, grp < G - 1], [grp < G - 1, grp > 0]
    partner = at(grp, pos + 1 - 2 * core)

    def grp_at(k):
        return lax.rem(grp + k, G)

    def chip_at(k):
        return lax.rem(chip + k, chips)

    locals_ = [
        pltpu.make_async_copy(obj_hbm, ext.at[:, pl.ds(HALO, TR), :], loc.at[0]),
        pltpu.make_async_copy(prb_hbm, prb, loc.at[1]),
        pltpu.make_async_copy(pat_hbm, pat, loc.at[2]),
        pltpu.make_async_copy(tab_hbm, tab, loc.at[3]),
    ]
    for c in locals_:
        c.start()

    barrier = pltpu.get_barrier_semaphore()
    for d in range(2):
        @pl.when(col_send[d])
        def _():
            pl.semaphore_signal(barrier, inc=1, **col_peer[d])
    for k in range(1, G):
        pl.semaphore_signal(barrier, inc=1, **at(grp_at(k), pos))
    for k in range(1, chips):
        pl.semaphore_signal(barrier, inc=1, **at(grp, chip_at(k) * 2 + core))
    pl.semaphore_signal(barrier, inc=1, **partner)
    expected = (pos > 0).astype(jnp.int32) + (pos < PN - 1).astype(jnp.int32) + G + chips - 1

    lane = lax.broadcasted_iota(jnp.int32, (M, HALO), 1)
    row8 = lax.broadcasted_iota(jnp.int32, (8, 128), 0)
    packed = jnp.zeros((8, 128), jnp.int32)
    for s in range(S):
        packed = jnp.where(row8 == s, corners[0, s] - grp * TR + HALO, packed)
    corv[...] = packed
    zero = jnp.zeros((HALO, HALO), jnp.float32)
    for s in range(S):
        for c in range(2):
            for at_row in (0, HALO + M):
                gmid[s, c, pl.ds(at_row, HALO), :] = zero
                for d in range(2):
                    grecv[d, s, c, pl.ds(at_row, HALO), :] = zero
    gp[...] = jnp.zeros(gp.shape, jnp.float32)

    pl.semaphore_wait(barrier, expected)

    def cor_copy(d):
        return pltpu.make_async_remote_copy(corv, cor_recv.at[d], corsem.at[0, d], corsem.at[1, d], **col_peer[d])

    def halo_copy(d):
        src, dst = ((0, HALO + TR), (TR - HALO, 0))[d]
        return pltpu.make_async_remote_copy(
            obj_hbm.at[:, pl.ds(src, HALO), :], ext.at[:, pl.ds(dst, HALO), :], yh.at[0, d], yh.at[1, d], **row_peer[d])

    for d in range(2):
        @pl.when(col_send[d])
        def _():
            cor_copy(d).start()

        @pl.when(row_send[d])
        def _():
            halo_copy(d).start()
    for d in range(2):
        @pl.when(col_recv[d])
        def _():
            cor_copy(d).wait_recv()
            c = pltpu.make_async_copy(cor_recv.at[d], cor_smem.at[d], cors.at[d])
            c.start()
            c.wait()
    locals_[0].wait()
    for d in range(2):
        @pl.when(row_recv[d])
        def _():
            halo_copy(d).wait_recv()

    def patch_copy(d, s):
        return pltpu.make_async_remote_copy(
            stage.at[d, s], nb.at[d, s], patsem.at[0, d, s], patsem.at[1, d, s], **col_peer[d])

    def grad_copy(d, s):
        return pltpu.make_async_remote_copy(
            gsend.at[d, s], grecv.at[d, s, :, pl.ds(HALO, M), :], gsem.at[0, d, s], gsem.at[1, d, s], **col_peer[d])

    def last_copy(d, c):
        return pltpu.make_async_remote_copy(
            gsend.at[d, S - 1, c], grecv.at[d, S - 1, c, pl.ds(HALO, M), :],
            gsem.at[0, d, S - 1 + c], gsem.at[1, d, S - 1 + c], **col_peer[d])

    for s in range(S):
        for d in range(2):
            @pl.when(col_send[d])
            def _():
                r = jnp.clip(cor_smem[1 - d, s, 0], 0, TR + 2 * HALO - M)
                for c in range(2):
                    stage[d, s, c] = ext[c, pl.ds(r, M), :]
                patch_copy(d, s).start()

    for c in locals_[1:]:
        c.wait()
    own_count = counts[grp * PN + pos]

    def slot(s, carry):
        r = jnp.clip(corners[0, s] - grp * TR + HALO, 0, TR + 2 * HALO - M)
        shift = jnp.clip(corners[1, s] - pos * HALO + HALO, 0, HALO)
        for d in range(2):
            @pl.when(col_recv[d])
            def _():
                patch_copy(d, s).wait_recv()
        back = lax.rem(HALO - shift, HALO)
        forth = lax.rem(shift, HALO)
        first = lane < HALO - shift
        patch = []
        for c in range(2):
            mid = pltpu.roll(ext[c, pl.ds(r, M), :], back, 1)
            before = pltpu.roll(nb[1, s, c], back, 1)
            after = pltpu.roll(nb[0, s, c], back, 1)
            patch.append(jnp.concatenate([jnp.where(first, before, mid), jnp.where(first, mid, after)], axis=1))
        pr, pi = prb[0], prb[1]
        wave = jnp.concatenate([pr * patch[0] - pi * patch[1], pr * patch[1] + pi * patch[0]], axis=0)
        front = table_left(tab, 0, wave)
        far = table_right(jnp.concatenate([front[:M], front[M:]], axis=1), tab, 1)
        fr, fi = far[:, :M], far[:, M:]
        excess = fr * fr + fi * fi - pat[s]
        excess = jnp.where(jnp.full((M, M), s, jnp.int32) < own_count, excess, 0.0)
        back_ = table_left(tab, 1, jnp.concatenate([excess * fr, excess * fi], axis=0))
        chi = table_right(jnp.concatenate([back_[:M], back_[M:]], axis=1), tab, 0)
        cr, ci = chi[:, :M], chi[:, M:]
        parts = (pr * cr + pi * ci, pr * ci - pi * cr)
        gp[0] += patch[0] * cr + patch[1] * ci
        gp[1] += patch[0] * ci - patch[1] * cr
        tail = lane >= shift
        for c in range(2):
            g0 = pltpu.roll(parts[c][:, :HALO], forth, 1)
            g1 = pltpu.roll(parts[c][:, HALO:], forth, 1)
            gsend[0, s, c] = jnp.where(tail, g0, 0.0)
            gmid[s, c, pl.ds(HALO, M), :] = jnp.where(tail, g1, g0)
            gsend[1, s, c] = jnp.where(tail, 0.0, g1)
        for d in range(2):
            @pl.when(col_send[d] & (s < S - 1))
            def _():
                grad_copy(d, s).start()
        return carry

    lax.fori_loop(0, S, slot, 0)

    core_copy = pltpu.make_async_remote_copy(
        gp.at[:, pl.ds((1 - core) * half, half), :], p1r, csem.at[0], csem.at[1], **partner)
    core_copy.start()
    core_copy.wait_recv()
    p1[...] = gp[:, pl.ds(pl.multiple_of(core * half, half), half), :] + p1r[...]

    def grp_copy(k):
        rows = pl.ds(pl.multiple_of(grp_at(k) * h2, h2), h2)
        return pltpu.make_async_remote_copy(
            p1.at[:, rows, :], p2r.at[k], gysem.at[0, k], gysem.at[1, k], **at(grp_at(k), pos))

    for k in range(1, G):
        grp_copy(k).start()

    for k in range(1, G):
        grp_copy(k).wait_recv()
    total = p1[:, pl.ds(pl.multiple_of(grp * h2, h2), h2), :]
    for k in range(1, G):
        total = total + p2r[k]
    p2[...] = total

    def share_copy(k):
        q = lax.rem(chip_at(k), owners)
        rows = pl.ds(pl.multiple_of(q * h3, 8), h3)
        return pltpu.make_async_remote_copy(
            p2.at[:, rows, :], p3r.at[k], asem.at[0, k], asem.at[1, k], **at(grp, chip_at(k) * 2 + core))

    for k in range(1, chips):
        @pl.when(chip_at(k) < owners)
        def _():
            share_copy(k).start()

    for d in range(2):
        @pl.when(col_send[d])
        def _():
            last_copy(d, 0).start()

    live = counts[0]
    for i in range(1, G * PN):
        live = live + counts[i]

    def new_rows(owner):
        return pl.ds(pl.multiple_of(core * half + grp * h2 + lax.rem(owner, owners) * h3, 8), h3)

    @pl.when(chip < owners)
    def _():
        total = p2[:, pl.ds(pl.multiple_of(lax.rem(chip, owners) * h3, 8), h3), :]
        for k in range(1, chips):
            share_copy(k).wait_recv()
            total = total + p3r[k]
        divisor = jnp.full(total.shape, live, jnp.int32).astype(jnp.float32)
        pnew[:, new_rows(chip), :] = prb[:, new_rows(chip), :] - STEP_PROBE * total / divisor

    def spread_copy(k, owner):
        return pltpu.make_async_remote_copy(
            pnew.at[:, new_rows(owner), :], pnew.at[:, new_rows(owner), :], agsem.at[0, k], agsem.at[1, k],
            **at(grp, chip_at(k) * 2 + core))

    @pl.when(chip < owners)
    def _():
        for k in range(1, chips):
            spread_copy(k, chip).start()
    for d in range(2):
        @pl.when(col_send[d])
        def _():
            last_copy(d, 1).start()

    for k in range(1, chips):
        source = lax.rem(chip + chips - k, chips)

        @pl.when(source < owners)
        def _():
            spread_copy(k, source).wait_recv()

    def grp_spread(k, g):
        rows = pl.ds(pl.multiple_of(core * half + g * h2, h2), h2)
        return pltpu.make_async_remote_copy(
            pnew.at[:, rows, :], pnew.at[:, rows, :], gasem.at[0, k], gasem.at[1, k], **at(grp_at(k), pos))

    for k in range(1, G):
        grp_spread(k, grp).start()

    for d in range(2):
        @pl.when(col_recv[d])
        def _():
            for s in range(S - 1):
                grad_copy(d, s).wait_recv()
            for c in range(2):
                last_copy(d, c).wait_recv()

    def gather(chunk, carry):
        base = pl.multiple_of(chunk * HALO, HALO)
        totals = [jnp.zeros((HALO, HALO), jnp.float32)] * 2
        for s in range(S):
            off = jnp.clip(base - (corners[0, s] - grp * TR + HALO) + HALO, 0, HALO + M)
            totals = [totals[c] + gmid[s, c, pl.ds(off, HALO), :] for c in range(2)]
        for c in range(2):
            gacc[c, pl.ds(base, HALO), :] = totals[c]
        for d in range(2):
            @pl.when(col_recv[d])
            def _():
                for c in range(2):
                    total = gacc[c, pl.ds(base, HALO), :]
                    for s in range(S):
                        off = jnp.clip(base - cor_smem[d, s, 0] + HALO, 0, HALO + M)
                        total = total + grecv[d, s, c, pl.ds(off, HALO), :]
                    gacc[c, pl.ds(base, HALO), :] = total
        return carry

    lax.fori_loop(0, (TR + 2 * HALO) // HALO, gather, 0)

    def rim_copy(d):
        src = (0, HALO + TR)[d]
        return pltpu.make_async_remote_copy(
            gacc.at[:, pl.ds(src, HALO), :], yrecv.at[d], ysem.at[0, d], ysem.at[1, d], **row_peer[d])

    for d in range(2):
        @pl.when(row_send[d])
        def _():
            rim_copy(d).start()

    for k in range(1, G):
        grp_spread(k, lax.rem(grp + G - k, G)).wait_recv()

    def core_spread(c):
        rows = pl.ds(pl.multiple_of(c * half, half), half)
        return pltpu.make_async_remote_copy(pnew.at[:, rows, :], pnew.at[:, rows, :], casem.at[0], casem.at[1], **partner)

    core_spread(core).start()

    obj_out[...] = ext[:, pl.ds(HALO, TR), :] - STEP_OBJECT * gacc[:, pl.ds(HALO, TR), :]
    for d in range(2):
        @pl.when(row_recv[d])
        def _():
            rim_copy(d).wait_recv()
            rows = pl.ds((TR - HALO, 0)[d], HALO)
            obj_out[:, rows, :] = obj_out[:, rows, :] - STEP_OBJECT * yrecv[d]

    core_spread(1 - core).wait_recv()
    prb_out[...] = pnew[...]

    for d in range(2):
        @pl.when(col_send[d])
        def _():
            cor_copy(d).wait_send()
            for c in range(2):
                last_copy(d, c).wait_send()
            for s in range(S):
                patch_copy(d, s).wait_send()
                if s < S - 1:
                    grad_copy(d, s).wait_send()

        @pl.when(row_send[d])
        def _():
            halo_copy(d).wait_send()
            rim_copy(d).wait_send()
    core_copy.wait_send()
    for k in range(1, G):
        grp_copy(k).wait_send()
        grp_spread(k, grp).wait_send()
    for k in range(1, chips):
        @pl.when(chip_at(k) < owners)
        def _():
            share_copy(k).wait_send()

        @pl.when(chip < owners)
        def _():
            spread_copy(k, chip).wait_send()
    core_spread(core).wait_send()


def on_device(grp_size, pos_size, tables, object_field, probe_field, patterns, corners, counts):
    TR, S, M = object_field.shape[1], patterns.shape[0], probe_field.shape[1]
    chips, half = pos_size // 2, M // 2
    h2 = half // grp_size
    h3 = max(8, h2 // chips)
    f32 = jnp.float32
    V, D = pltpu.VMEM, pltpu.SemaphoreType.DMA
    smem = pl.BlockSpec(memory_space=pltpu.SMEM)
    hbm = pl.BlockSpec(memory_space=pl.ANY)
    vmem = pl.BlockSpec(memory_space=pltpu.VMEM)
    return pl.pallas_call(
        functools.partial(kernel, (grp_size, pos_size, S, TR, M)),
        out_shape=(
            pltpu.VMEM(object_field.shape, f32),
            pltpu.VMEM(probe_field.shape, f32),
        ),
        in_specs=[smem, smem, hbm, hbm, hbm, hbm],
        out_specs=(vmem, vmem),
        scratch_shapes=[
            V((2, TR + 2 * HALO, HALO), f32),
            V((2, M, M), f32),
            V((S, M, M), f32),
            V(tables.shape, jnp.bfloat16),
            V((2, S, 2, M, HALO), f32),
            V((2, S, 2, M, HALO), f32),
            V((8, 128), jnp.int32),
            V((2, 8, 128), jnp.int32),
            pltpu.SMEM((2, 8, 128), jnp.int32),
            V((S, 2, M + 2 * HALO, HALO), f32),
            V((2, S, 2, M, HALO), f32),
            V((2, S, 2, M + 2 * HALO, HALO), f32),
            V((2, TR + 2 * HALO, HALO), f32),
            V((2, 2, HALO, HALO), f32),
            V((2, M, M), f32),
            V((2, half, M), f32),
            V((2, half, M), f32),
            V((grp_size, 2, h2, M), f32),
            V((2, h2, M), f32),
            V((chips, 2, h3, M), f32),
            V((2, M, M), f32),
            D((4,)), D((2, 2)), D((2, 2)), D((2,)), D((2, 2, S)), D((2, 2, S + 1)), D((2, 2)), D((2,)),
            D((2, grp_size)), D((2, chips)), D((2, chips)), D((2, grp_size)), D((2,)),
        ],
        compiler_params=pltpu.CompilerParams(
            collective_id=0, has_side_effects=True, vmem_limit_bytes=56 * 1024 * 1024
        ),
    )(corners, counts, object_field, probe_field, patterns, jnp.asarray(tables))


def solution(mesh):
    def body(object_field, probe_field, patterns, corners, counts):
        tables = dft_tables(probe_field.shape[1])
        return on_device(
            mesh.shape["grp"], mesh.shape["pos"], tables, object_field, probe_field, patterns, corners, counts
        )

    return jax.shard_map(
        body,
        mesh=mesh,
        in_specs=(
            P(None, "grp", "pos"),
            P(),
            P(("grp", "pos"), None, None),
            P(None, ("grp", "pos")),
            P(),
        ),
        out_specs=(P(None, "grp", "pos"), P()),
        check_vma=False,
    )
```

```python
import functools

import jax
import jax.numpy as jnp
import numpy as np
from jax import lax
from jax.experimental import pallas as pl
from jax.experimental.pallas import tpu as pltpu
from jax.sharding import PartitionSpec as P

HALO = 128
STEP_OBJECT = 0.25
STEP_PROBE = 4.0
MESH = pl.DeviceIdType.MESH


def dft_tables(order):
    indices = np.arange(order, dtype=np.int64)
    angles = (indices[:, None] * indices[None, :] % order) * (2.0 * np.pi / order)
    cos = np.cos(angles) / np.sqrt(order)
    sin = -np.sin(angles) / np.sqrt(order)
    left = np.block([[cos, -sin], [sin, cos]])
    right = np.block([[cos, sin], [-sin, cos]])
    both = np.stack([left, right]).astype(np.float32)
    high = both.astype(jnp.bfloat16)
    low = (both - high.astype(np.float32)).astype(jnp.bfloat16)
    return np.stack([high, low], axis=1)


def split(x):
    high = x.astype(jnp.bfloat16)
    low = (x - high.astype(jnp.float32)).astype(jnp.bfloat16)
    return high, low


def dot(a, b):
    return jnp.dot(a, b, preferred_element_type=jnp.float32)


def table_left(tab, which, data):
    high, low = split(data)
    th, tl = tab[which, 0], tab[which, 1]
    return dot(th, high) + (dot(th, low) + dot(tl, high))


def table_right(data, tab, which):
    high, low = split(data)
    th, tl = tab[which, 0], tab[which, 1]
    return dot(high, th) + (dot(low, th) + dot(high, tl))


def kernel(sizes, corners, counts, obj_hbm, prb_hbm, pat_hbm, tab_hbm, obj_out, prb_out,
           ext, prb, pat, tab, nb, stage, corv, cor_recv, cor_smem,
           gmid, gsend, grecv, gacc, yrecv, gp, p1r, p1, p2r, p2, p3r, pnew,
           loc, yh, corsem, cors, patsem, gsem, ysem, csem, gysem, asem, agsem, gasem, casem):
    G, PN, S, TR, M = sizes
    grp, pos = lax.axis_index("grp"), lax.axis_index("pos")
    core, chip, chips = lax.rem(pos, 2), pos // 2, PN // 2
    half = M // 2
    h2 = half // G
    h3 = max(8, h2 // chips)
    owners = h2 // h3

    def at(g, p):
        return {"device_id": (g, p), "device_id_type": MESH}

    col_peer = [at(grp, lax.rem(pos + PN - 1, PN)), at(grp, lax.rem(pos + 1, PN))]
    row_peer = [at(lax.rem(grp + G - 1, G), pos), at(lax.rem(grp + 1, G), pos)]
    col_send, col_recv = [pos > 0, pos < PN - 1], [pos < PN - 1, pos > 0]
    row_send, row_recv = [grp > 0, grp < G - 1], [grp < G - 1, grp > 0]
    partner = at(grp, pos + 1 - 2 * core)

    def grp_at(k):
        return lax.rem(grp + k, G)

    def chip_at(k):
        return lax.rem(chip + k, chips)

    locals_ = [
        pltpu.make_async_copy(obj_hbm, ext.at[:, pl.ds(HALO, TR), :], loc.at[0]),
        pltpu.make_async_copy(prb_hbm, prb, loc.at[1]),
        pltpu.make_async_copy(pat_hbm, pat, loc.at[2]),
        pltpu.make_async_copy(tab_hbm, tab, loc.at[3]),
    ]
    for c in locals_:
        c.start()

    barrier = pltpu.get_barrier_semaphore()
    for d in range(2):
        @pl.when(col_send[d])
        def _():
            pl.semaphore_signal(barrier, inc=1, **col_peer[d])
    for k in range(1, G):
        pl.semaphore_signal(barrier, inc=1, **at(grp_at(k), pos))
    for k in range(1, chips):
        pl.semaphore_signal(barrier, inc=1, **at(grp, chip_at(k) * 2 + core))
    pl.semaphore_signal(barrier, inc=1, **partner)
    expected = (pos > 0).astype(jnp.int32) + (pos < PN - 1).astype(jnp.int32) + G + chips - 1

    lane = lax.broadcasted_iota(jnp.int32, (M, HALO), 1)
    row8 = lax.broadcasted_iota(jnp.int32, (8, 128), 0)
    packed = jnp.zeros((8, 128), jnp.int32)
    for s in range(S):
        packed = jnp.where(row8 == s, corners[0, s] - grp * TR + HALO, packed)
    corv[...] = packed
    zero = jnp.zeros((HALO, HALO), jnp.float32)
    for s in range(S):
        for c in range(2):
            for at_row in (0, HALO + M):
                gmid[s, c, pl.ds(at_row, HALO), :] = zero
                for d in range(2):
                    grecv[d, s, c, pl.ds(at_row, HALO), :] = zero
    gp[...] = jnp.zeros(gp.shape, jnp.float32)

    pl.semaphore_wait(barrier, expected)

    def cor_copy(d):
        return pltpu.make_async_remote_copy(corv, cor_recv.at[d], corsem.at[0, d], corsem.at[1, d], **col_peer[d])

    def halo_copy(d):
        src, dst = ((0, HALO + TR), (TR - HALO, 0))[d]
        return pltpu.make_async_remote_copy(
            obj_hbm.at[:, pl.ds(src, HALO), :], ext.at[:, pl.ds(dst, HALO), :], yh.at[0, d], yh.at[1, d], **row_peer[d])

    for d in range(2):
        @pl.when(col_send[d])
        def _():
            cor_copy(d).start()

        @pl.when(row_send[d])
        def _():
            halo_copy(d).start()
    for d in range(2):
        @pl.when(col_recv[d])
        def _():
            cor_copy(d).wait_recv()
            c = pltpu.make_async_copy(cor_recv.at[d], cor_smem.at[d], cors.at[d])
            c.start()
            c.wait()
    locals_[0].wait()
    for d in range(2):
        @pl.when(row_recv[d])
        def _():
            halo_copy(d).wait_recv()

    def patch_copy(d, s):
        return pltpu.make_async_remote_copy(
            stage.at[d, s], nb.at[d, s], patsem.at[0, d, s], patsem.at[1, d, s], **col_peer[d])

    def grad_copy(d, s, c):
        return pltpu.make_async_remote_copy(
            gsend.at[d, s, c], grecv.at[d, s, c, pl.ds(HALO, M), :],
            gsem.at[0, d, s, c], gsem.at[1, d, s, c], **col_peer[d])

    for s in range(S):
        for d in range(2):
            @pl.when(col_send[d])
            def _():
                r = jnp.clip(cor_smem[1 - d, s, 0], 0, TR + 2 * HALO - M)
                for c in range(2):
                    stage[d, s, c] = ext[c, pl.ds(r, M), :]
                patch_copy(d, s).start()

    for c in locals_[1:]:
        c.wait()
    own_count = counts[grp * PN + pos]

    def slot(s, carry):
        r = jnp.clip(corners[0, s] - grp * TR + HALO, 0, TR + 2 * HALO - M)
        shift = jnp.clip(corners[1, s] - pos * HALO + HALO, 0, HALO)
        for d in range(2):
            @pl.when(col_recv[d])
            def _():
                patch_copy(d, s).wait_recv()
        back = lax.rem(HALO - shift, HALO)
        forth = lax.rem(shift, HALO)
        first = lane < HALO - shift
        patch = []
        for c in range(2):
            mid = pltpu.roll(ext[c, pl.ds(r, M), :], back, 1)
            before = pltpu.roll(nb[1, s, c], back, 1)
            after = pltpu.roll(nb[0, s, c], back, 1)
            patch.append(jnp.concatenate([jnp.where(first, before, mid), jnp.where(first, mid, after)], axis=1))
        pr, pi = prb[0], prb[1]
        wave = jnp.concatenate([pr * patch[0] - pi * patch[1], pr * patch[1] + pi * patch[0]], axis=0)
        front = table_left(tab, 0, wave)
        far = table_right(jnp.concatenate([front[:M], front[M:]], axis=1), tab, 1)
        fr, fi = far[:, :M], far[:, M:]
        excess = fr * fr + fi * fi - pat[s]
        excess = jnp.where(jnp.full((M, M), s, jnp.int32) < own_count, excess, 0.0)
        back_ = table_left(tab, 1, jnp.concatenate([excess * fr, excess * fi], axis=0))
        chi = table_right(jnp.concatenate([back_[:M], back_[M:]], axis=1), tab, 0)
        cr, ci = chi[:, :M], chi[:, M:]
        parts = (pr * cr + pi * ci, pr * ci - pi * cr)
        gp[0] += patch[0] * cr + patch[1] * ci
        gp[1] += patch[0] * ci - patch[1] * cr
        tail = lane >= shift
        for c in range(2):
            g0 = pltpu.roll(parts[c][:, :HALO], forth, 1)
            g1 = pltpu.roll(parts[c][:, HALO:], forth, 1)
            gsend[0, s, c] = jnp.where(tail, g0, 0.0)
            gmid[s, c, pl.ds(HALO, M), :] = jnp.where(tail, g1, g0)
            gsend[1, s, c] = jnp.where(tail, 0.0, g1)
        for d in range(2):
            @pl.when(col_send[d] & (s < S - 1))
            def _():
                grad_copy(d, s, 0).start()

            @pl.when(col_send[d] & (s < S - 2))
            def _():
                grad_copy(d, s, 1).start()
        return carry

    lax.fori_loop(0, S, slot, 0)

    core_copy = pltpu.make_async_remote_copy(
        gp.at[:, pl.ds((1 - core) * half, half), :], p1r, csem.at[0], csem.at[1], **partner)
    core_copy.start()
    core_copy.wait_recv()
    p1[...] = gp[:, pl.ds(pl.multiple_of(core * half, half), half), :] + p1r[...]

    def grp_copy(k):
        rows = pl.ds(pl.multiple_of(grp_at(k) * h2, h2), h2)
        return pltpu.make_async_remote_copy(
            p1.at[:, rows, :], p2r.at[k], gysem.at[0, k], gysem.at[1, k], **at(grp_at(k), pos))

    for k in range(1, G):
        grp_copy(k).start()

    for k in range(1, G):
        grp_copy(k).wait_recv()
    total = p1[:, pl.ds(pl.multiple_of(grp * h2, h2), h2), :]
    for k in range(1, G):
        total = total + p2r[k]
    p2[...] = total

    def share_copy(k):
        q = lax.rem(chip_at(k), owners)
        rows = pl.ds(pl.multiple_of(q * h3, 8), h3)
        return pltpu.make_async_remote_copy(
            p2.at[:, rows, :], p3r.at[k], asem.at[0, k], asem.at[1, k], **at(grp, chip_at(k) * 2 + core))

    for k in range(1, chips):
        @pl.when(chip_at(k) < owners)
        def _():
            share_copy(k).start()

    for d in range(2):
        @pl.when(col_send[d])
        def _():
            if S > 1:
                grad_copy(d, S - 2, 1).start()

    live = counts[0]
    for i in range(1, G * PN):
        live = live + counts[i]

    def new_rows(owner):
        return pl.ds(pl.multiple_of(core * half + grp * h2 + lax.rem(owner, owners) * h3, 8), h3)

    @pl.when(chip < owners)
    def _():
        total = p2[:, pl.ds(pl.multiple_of(lax.rem(chip, owners) * h3, 8), h3), :]
        for k in range(1, chips):
            share_copy(k).wait_recv()
            total = total + p3r[k]
        divisor = jnp.full(total.shape, live, jnp.int32).astype(jnp.float32)
        pnew[:, new_rows(chip), :] = prb[:, new_rows(chip), :] - STEP_PROBE * total / divisor

    def spread_copy(k, owner):
        return pltpu.make_async_remote_copy(
            pnew.at[:, new_rows(owner), :], pnew.at[:, new_rows(owner), :], agsem.at[0, k], agsem.at[1, k],
            **at(grp, chip_at(k) * 2 + core))

    @pl.when(chip < owners)
    def _():
        for k in range(1, chips):
            spread_copy(k, chip).start()
    for d in range(2):
        @pl.when(col_send[d])
        def _():
            for c in range(2):
                grad_copy(d, S - 1, c).start()

    for k in range(1, chips):
        source = lax.rem(chip + chips - k, chips)

        @pl.when(source < owners)
        def _():
            spread_copy(k, source).wait_recv()

    def grp_spread(k, g):
        rows = pl.ds(pl.multiple_of(core * half + g * h2, h2), h2)
        return pltpu.make_async_remote_copy(
            pnew.at[:, rows, :], pnew.at[:, rows, :], gasem.at[0, k], gasem.at[1, k], **at(grp_at(k), pos))

    for k in range(1, G):
        grp_spread(k, grp).start()

    for d in range(2):
        @pl.when(col_recv[d])
        def _():
            for s in range(S):
                for c in range(2):
                    grad_copy(d, s, c).wait_recv()

    def gather(base):
        totals = [jnp.zeros((HALO, HALO), jnp.float32)] * 2
        for s in range(S):
            off = jnp.clip(base - (corners[0, s] - grp * TR + HALO) + HALO, 0, HALO + M)
            totals = [totals[c] + gmid[s, c, pl.ds(off, HALO), :] for c in range(2)]
        for c in range(2):
            gacc[c, pl.ds(base, HALO), :] = totals[c]
        for d in range(2):
            @pl.when(col_recv[d])
            def _():
                for c in range(2):
                    total = gacc[c, pl.ds(base, HALO), :]
                    for s in range(S):
                        off = jnp.clip(base - cor_smem[d, s, 0] + HALO, 0, HALO + M)
                        total = total + grecv[d, s, c, pl.ds(off, HALO), :]
                    gacc[c, pl.ds(base, HALO), :] = total

    def gather_rim(chunk, carry):
        gather(pl.multiple_of(chunk * (TR + HALO), HALO))
        return carry

    def gather_core(chunk, carry):
        base = pl.multiple_of(chunk * HALO + HALO, HALO)
        gather(base)
        for c in range(2):
            obj_out[c, pl.ds(pl.multiple_of(chunk * HALO, HALO), HALO), :] = (
                ext[c, pl.ds(base, HALO), :] - STEP_OBJECT * gacc[c, pl.ds(base, HALO), :])
        return carry

    lax.fori_loop(0, 2, gather_rim, 0)

    def rim_copy(d):
        src = (0, HALO + TR)[d]
        return pltpu.make_async_remote_copy(
            gacc.at[:, pl.ds(src, HALO), :], yrecv.at[d], ysem.at[0, d], ysem.at[1, d], **row_peer[d])

    for d in range(2):
        @pl.when(row_send[d])
        def _():
            rim_copy(d).start()

    for k in range(1, G):
        grp_spread(k, lax.rem(grp + G - k, G)).wait_recv()

    def core_spread(c):
        rows = pl.ds(pl.multiple_of(c * half, half), half)
        return pltpu.make_async_remote_copy(pnew.at[:, rows, :], pnew.at[:, rows, :], casem.at[0], casem.at[1], **partner)

    core_spread(core).start()

    lax.fori_loop(0, TR // HALO, gather_core, 0)
    for d in range(2):
        @pl.when(row_recv[d])
        def _():
            rim_copy(d).wait_recv()
            rows = pl.ds((TR - HALO, 0)[d], HALO)
            obj_out[:, rows, :] = obj_out[:, rows, :] - STEP_OBJECT * yrecv[d]

    core_spread(1 - core).wait_recv()
    prb_out[...] = pnew[...]

    for d in range(2):
        @pl.when(col_send[d])
        def _():
            cor_copy(d).wait_send()
            for s in range(S):
                patch_copy(d, s).wait_send()
                for c in range(2):
                    grad_copy(d, s, c).wait_send()

        @pl.when(row_send[d])
        def _():
            halo_copy(d).wait_send()
            rim_copy(d).wait_send()
    core_copy.wait_send()
    for k in range(1, G):
        grp_copy(k).wait_send()
        grp_spread(k, grp).wait_send()
    for k in range(1, chips):
        @pl.when(chip_at(k) < owners)
        def _():
            share_copy(k).wait_send()

        @pl.when(chip < owners)
        def _():
            spread_copy(k, chip).wait_send()
    core_spread(core).wait_send()


def on_device(grp_size, pos_size, tables, object_field, probe_field, patterns, corners, counts):
    TR, S, M = object_field.shape[1], patterns.shape[0], probe_field.shape[1]
    chips, half = pos_size // 2, M // 2
    h2 = half // grp_size
    h3 = max(8, h2 // chips)
    f32 = jnp.float32
    V, D = pltpu.VMEM, pltpu.SemaphoreType.DMA
    smem = pl.BlockSpec(memory_space=pltpu.SMEM)
    hbm = pl.BlockSpec(memory_space=pl.ANY)
    vmem = pl.BlockSpec(memory_space=pltpu.VMEM)
    return pl.pallas_call(
        functools.partial(kernel, (grp_size, pos_size, S, TR, M)),
        out_shape=(
            pltpu.VMEM(object_field.shape, f32),
            pltpu.VMEM(probe_field.shape, f32),
        ),
        in_specs=[smem, smem, hbm, hbm, hbm, hbm],
        out_specs=(vmem, vmem),
        scratch_shapes=[
            V((2, TR + 2 * HALO, HALO), f32),
            V((2, M, M), f32),
            V((S, M, M), f32),
            V(tables.shape, jnp.bfloat16),
            V((2, S, 2, M, HALO), f32),
            V((2, S, 2, M, HALO), f32),
            V((8, 128), jnp.int32),
            V((2, 8, 128), jnp.int32),
            pltpu.SMEM((2, 8, 128), jnp.int32),
            V((S, 2, M + 2 * HALO, HALO), f32),
            V((2, S, 2, M, HALO), f32),
            V((2, S, 2, M + 2 * HALO, HALO), f32),
            V((2, TR + 2 * HALO, HALO), f32),
            V((2, 2, HALO, HALO), f32),
            V((2, M, M), f32),
            V((2, half, M), f32),
            V((2, half, M), f32),
            V((grp_size, 2, h2, M), f32),
            V((2, h2, M), f32),
            V((chips, 2, h3, M), f32),
            V((2, M, M), f32),
            D((4,)), D((2, 2)), D((2, 2)), D((2,)), D((2, 2, S)), D((2, 2, S, 2)), D((2, 2)), D((2,)),
            D((2, grp_size)), D((2, chips)), D((2, chips)), D((2, grp_size)), D((2,)),
        ],
        compiler_params=pltpu.CompilerParams(
            collective_id=0, has_side_effects=True, vmem_limit_bytes=56 * 1024 * 1024
        ),
    )(corners, counts, object_field, probe_field, patterns, jnp.asarray(tables))


def solution(mesh):
    def body(object_field, probe_field, patterns, corners, counts):
        tables = dft_tables(probe_field.shape[1])
        return on_device(
            mesh.shape["grp"], mesh.shape["pos"], tables, object_field, probe_field, patterns, corners, counts
        )

    return jax.shard_map(
        body,
        mesh=mesh,
        in_specs=(
            P(None, "grp", "pos"),
            P(),
            P(("grp", "pos"), None, None),
            P(None, ("grp", "pos")),
            P(),
        ),
        out_specs=(P(None, "grp", "pos"), P()),
        check_vma=False,
    )
```
